32 devices in a mesh: groups: 2 (over y), blk: 4 (over z), side: 2 (over x), tp: 2 (over core).
Axes of the slice: x: 2, y: 2, z: 4, core: 2. Of those that a mesh axis runs over, the one named last changes fastest.
Arguments:
- queries: bfloat16 [4, 512, 4096], P(('groups', 'side'), 'blk', 'tp'), parts along dimension 0, may hold values from -8 to 8
- key_rows: bfloat16 [4, 512, 256], P(('groups', 'side'), 'blk', 'tp'), parts along dimension 0, may hold values from -8 to 8
- value_rows: bfloat16 [4, 512, 256], P(('groups', 'side'), 'blk', 'tp'), parts along dimension 0, may hold values from -6 to 6
- segments: int32 [4, 512], P(('groups', 'side'), 'blk'), parts along dimension 0, may hold values from 0 to 1, never falling along the last dimension, each value on 1 to 384 neighbouring positions
- hidden_entry_rows: bfloat16 [4, 512, 4096], P(('groups', 'side'), 'blk', 'tp'), parts along dimension 0, may hold values from -6 to 6
- expert_ids: int32 [4, 512, 8], P(('groups', 'side'), 'blk'), parts along dimension 0, may hold values from 0 to 127, all different within a row; in each aligned block of 128 rows (0 to 127, 128 to 255, ..., all dimensions but the last counted through in order) at most 10 rows name the same one
- route_weight: float32 [4, 512, 8], P(('groups', 'side'), 'blk'), parts along dimension 0, may hold values from 0.2 to 1
- w_gate: bfloat16 [4, 2048, 1536], P('blk', 'tp', 'side'), may hold values from -0.09375 to 0.09375
- w_up: bfloat16 [4, 2048, 1536], P('blk', 'tp', 'side'), may hold values from -0.09375 to 0.09375
- w_down: bfloat16 [4, 1536, 2048], P('blk', 'side', 'tp'), may hold values from -0.15625 to 0.15625
Outputs:
- attended: bfloat16 [4, 512, 4096], P(('groups', 'side'), 'blk', 'tp'), parts along dimension 0
- moe_out: bfloat16 [4, 512, 4096], P(('groups', 'side'), 'blk', 'tp'), parts along dimension 0
The draws below stay inside these ranges and needn't reach their ends.
There are 2 independent parts, one for each index of `groups`. The reference program is written for one: setup_inputs(seed, part) draws one part's arguments, and reference() takes and returns one part's arrays. A program takes and returns all parts, laid end to end along the dimension named above; an argument that names none is the same for every part. Nothing has to cross between parts.
Inputs may be any that keep to these rules, and one draw needn't show every extreme that they name: `expert_ids`: in the 128 rows of one device (aligned blocks of rows of a sequence) no expert is named by more than 10 rows, and in some such block one is named by exactly 10; a row names 8 different experts. `segments`: document numbers never fall along a sequence; a document spans at most 384 positions, and one spans exactly that many.
All inputs are finite; a program needn't handle non-finite values.
Results may differ from the reference program's by a relative error of at most 0.02.
Values may be sent and summed in bfloat16 or wider, within the bound.
A program may use at most 64 MiB of HBM per device.

```python
import math
import jax
import jax.numpy as jnp
import numpy as np
from jax import lax

D = 4096
FF = 1536
ALL_EXPERTS = 128
TOPK = 8
HEAD_DIM = 128
HEADS = 32
KV_HEADS = 2
TOK_DEV = 128
SEQ_LEN = 512
SEQS = 2
EXPERTS = 2
D_QUARTER = 1024
FF_PART = 768
CAP = 10
DOCS = 2
LONGEST = 384
N_BLK = 4
N_SIDE = 2
N_TP = 2


def paired_draw(key):
    base = jax.random.fold_in(key, 7)
    first, second = jax.random.split(base, 2)
    query_all = jnp.clip(jax.random.normal(first, (SEQS, SEQ_LEN, HEADS, HEAD_DIM), jnp.float32), -6.0, 6.0)
    key_all = jnp.clip(jax.random.normal(second, (SEQS, SEQ_LEN, KV_HEADS, HEAD_DIM), jnp.float32), -6.0, 6.0)
    return (query_all.reshape(SEQS, SEQ_LEN, HEADS * HEAD_DIM), key_all.reshape(SEQS, SEQ_LEN, KV_HEADS * HEAD_DIM))


def draw_queries(key, part):
    return paired_draw(key)[0].astype(jnp.bfloat16)


def draw_key_rows(key, part):
    return paired_draw(key)[1].astype(jnp.bfloat16)


def block_scale(key, shape, shards, least, largest):
    gain = 1.0
    for axis_at, shards_of in shards:
        draws = jax.random.uniform(jax.random.fold_in(jax.random.fold_in(key, 6), axis_at), (shards_of,), jnp.float32, least / len(shards), largest / len(shards))
        gain = gain * jnp.repeat(jnp.exp(draws), shape[axis_at] // shards_of).reshape((-1,) + (1,) * (len(shape) - 1 - axis_at))
    return gain


def split_up(amount, total, limit, slope):
    weights = [(1 << 20) // math.isqrt(rank ** slope) + 1 for rank in range(2, amount + 1)]
    spare, given = total - limit - (amount - 1), [1] * (amount - 1)
    while spare > 0:
        candidates = [i for i in range(amount - 1) if given[i] < limit]
        whole, budget = sum([weights[i] for i in candidates]), spare
        for i in candidates:
            more = min(limit - given[i], max(1, budget * weights[i] // whole), spare)
            given[i] = given[i] + more
            spare = spare - more
    return np.array([limit] + given)


def uneven(stream_key, amount, total, limit, slope):
    if amount == 2:
        one = jax.random.randint(stream_key, (), max(1, total - limit), min(limit, total - 1) + 1)
        return jnp.stack([one, total - one])
    sizes = jnp.asarray(split_up(amount, total, limit, slope), jnp.int32)
    pairs = (amount - 1) // 2
    source_of, receiver = sizes[1:1 + 2 * pairs:2], sizes[2:2 + 2 * pairs:2]
    slack = jnp.minimum(source_of - 1, limit - receiver)
    passed = jax.random.randint(jax.random.fold_in(stream_key, 1), (pairs,), 0, 1 << 20) % (slack + 1)
    sizes = sizes.at[1:1 + 2 * pairs:2].set(source_of - passed).at[2:2 + 2 * pairs:2].set(receiver + passed)
    return sizes[jax.random.permutation(jax.random.fold_in(stream_key, 2), amount)]


def assign_block(key, own, number, rows, amount, top, most, slope):
    order = jax.random.permutation(key, amount)
    crowded, common = load_shares(amount, rows * top, most, slope, True), load_shares(amount, rows * top, most, slope, False)
    places = jnp.arange(amount)

    def named(lengths, offset_by):
        used = int((lengths > 0).sum())
        fixed = max(1, used // 4)
        shifted = fixed + (places - fixed + offset_by * (used - fixed)) % max(1, amount - fixed)
        return jnp.zeros((amount,), jnp.int32).at[order[jnp.where(places < fixed, places, shifted)]].set(jnp.asarray(lengths, jnp.int32))

    lengths = jnp.where(number % 4 == 0, named(crowded, number // 4), named(common, number - number // 4 - 1))
    mixed = jax.random.permutation(jax.random.fold_in(own, 3), amount)
    donor, receiver = mixed[0:amount // 2 * 2:2], mixed[1:amount // 2 * 2:2]
    slack = jnp.minimum(lengths[donor] - 1, most - lengths[receiver]) // 2
    slack = jnp.where((donor == order[0]) | (receiver == order[0]) | (lengths[receiver] == 0), 0, jnp.maximum(slack, 0))
    shifted = jax.random.randint(jax.random.fold_in(own, 4), (amount // 2,), 0, 1 << 20) % (slack + 1)
    lengths = lengths.at[donor].add(-shifted).at[receiver].add(shifted)
    items = jnp.searchsorted(jnp.cumsum(lengths), jnp.arange(rows * top), side="right").astype(jnp.int32)
    table = items.reshape(top, rows).T
    table = table[jax.random.permutation(jax.random.fold_in(own, 1), rows)]
    offset_by = jax.random.randint(jax.random.fold_in(own, 2), (rows, 1), 0, top)
    return jnp.take_along_axis(table, (jnp.arange(top)[None, :] + offset_by) % top, axis=1)


def load_shares(amount, total, most, lean, full):
    weights = [(1 << 20) // math.isqrt(rank ** lean) + 1 for rank in range(1, amount + 1)]
    largest = most if full else min(most, max(-(-total // amount), total * weights[0] // sum(weights)))
    least = 1 if total - largest >= amount - 1 else 0
    counts, spare = [largest] + [least] * (amount - 1), total - largest - least * (amount - 1)
    while spare > 0:
        movable = [i for i in range(1, amount) if counts[i] < largest] or [i for i in range(1, amount) if counts[i] < most]
        whole, left = sum([weights[i] for i in movable]), spare
        for i in movable:
            extra = min(most - counts[i], max(1, left * weights[i] // whole), spare)
            counts[i] = counts[i] + extra
            spare = spare - extra
    return np.array(counts)


def centred(key, extent, spread, most, cuts=(), kind=jnp.bfloat16):
    factor_of = block_scale(key, extent, cuts, -0.22, 0.18) if cuts else 1.0
    result = jax.random.normal(key, extent, jnp.float32) * spread * factor_of
    return jnp.minimum(jnp.maximum(result, -most), most).astype(kind)


def setup_inputs(seed: int = 0, part: int = 0) -> dict:
    splits = jax.random.split(jax.random.key(seed), 11)
    part_keys = jax.random.split(jax.random.fold_in(splits[10], part), 11)
    queries = draw_queries(jax.random.fold_in(jax.random.fold_in(splits[10], part), 71), part)
    key_rows = draw_key_rows(jax.random.fold_in(jax.random.fold_in(splits[10], part), 71), part)
    value_rows = centred(part_keys[2], (SEQS, SEQ_LEN, KV_HEADS * HEAD_DIM), 1.0, 6.0, ((0, 2), (1, 4), (2, 2)))
    segments = jax.vmap(lambda own: jnp.searchsorted(jnp.cumsum(uneven(own, DOCS, SEQ_LEN, LONGEST, 2)), jnp.arange(SEQ_LEN), side="right"))(jax.random.split(part_keys[3], SEQS)).reshape((SEQS, SEQ_LEN)).astype(jnp.int32)
    hidden_entry_rows = centred(part_keys[4], (SEQS, SEQ_LEN, D), 1.0, 6.0, ((0, 2), (1, 4), (2, 2)))
    expert_ids_keys = jax.random.split(jax.random.fold_in(part_keys[5], 1), SEQS * SEQ_LEN // TOK_DEV)
    expert_ids_turns = jax.random.permutation(jax.random.fold_in(part_keys[5], 3), SEQS * SEQ_LEN // TOK_DEV)
    expert_ids = jax.vmap(lambda own, number: assign_block(jax.random.fold_in(part_keys[5], 2), own, number, TOK_DEV, ALL_EXPERTS, TOPK, CAP, 1))(expert_ids_keys, expert_ids_turns).reshape((SEQS, SEQ_LEN, TOPK))
    route_weight = jnp.clip(0.2 + 0.8 * jax.random.uniform(part_keys[6], (SEQS, SEQ_LEN, TOPK), jnp.float32) ** block_scale(part_keys[6], (SEQS, SEQ_LEN, TOPK), ((0, 2), (1, 4)), -0.2, 0.2), 0.2, 1.0)
    w_gate = centred(splits[7], (2 * EXPERTS, D // 2, FF), D ** -0.5, 0.09375, ((0, 4), (1, 2), (2, 2)))
    w_up = centred(splits[8], (2 * EXPERTS, D // 2, FF), D ** -0.5, 0.09375, ((0, 4), (1, 2), (2, 2)))
    w_down = centred(splits[9], (2 * EXPERTS, FF, D // 2), FF ** -0.5, 0.15625, ((0, 4), (1, 2), (2, 2)))
    return {"queries": queries, "key_rows": key_rows, "value_rows": value_rows, "segments": segments, "hidden_entry_rows": hidden_entry_rows, "expert_ids": expert_ids, "route_weight": route_weight, "w_gate": w_gate, "w_up": w_up, "w_down": w_down}


def attend_sequence(operands):
    query_rows, key_rows, value_rows, segment_ids = operands
    length = query_rows.shape[0]
    group = HEADS // KV_HEADS
    query_portion = query_rows.reshape(length, HEADS, HEAD_DIM)
    key_split = key_rows.reshape(length, KV_HEADS, HEAD_DIM)
    value_split = value_rows.reshape(length, KV_HEADS, HEAD_DIM)
    positions = jnp.arange(length, dtype=jnp.int32)
    allowed = (positions[None, :] <= positions[:, None]) & (segment_ids[None, :] == segment_ids[:, None])
    factor = 1.0 / math.sqrt(HEAD_DIM)

    def one_head(head):
        query_head = lax.dynamic_index_in_dim(query_portion, head, 1, keepdims=False)
        key_head = lax.dynamic_index_in_dim(key_split, head // group, 1, keepdims=False)
        value_head = lax.dynamic_index_in_dim(value_split, head // group, 1, keepdims=False)
        scores = jnp.dot(query_head, key_head.T, preferred_element_type=jnp.float32) * factor
        scores = jnp.where(allowed, scores, -1e+30)
        row_max = lax.optimization_barrier(jnp.max(scores, axis=1, keepdims=True))
        weights = jnp.where(allowed, jnp.exp(scores - row_max), 0.0)
        totals = lax.optimization_barrier(jnp.sum(weights, axis=1, keepdims=True))
        mixed = jnp.dot(weights.astype(jnp.bfloat16), value_head, preferred_element_type=jnp.float32)
        return (mixed / totals).astype(jnp.bfloat16)
    heads_out = lax.map(one_head, jnp.arange(HEADS, dtype=jnp.int32))
    return jnp.transpose(heads_out, (1, 0, 2)).reshape(length, HEADS * HEAD_DIM)

def expert_pair(rows, gate_pair, up_pair, down_weight_couple):
    count = rows.shape[0]
    rows_split = rows.astype(jnp.float32).reshape(count, N_TP, 2, D_QUARTER)
    gate_split = gate_pair.astype(jnp.float32).reshape(2, N_TP, D_QUARTER, FF)
    up_split = up_pair.astype(jnp.float32).reshape(2, N_TP, D_QUARTER, FF)
    gate_terms = jnp.einsum('rtkq,ktqf->rtkf', rows_split, gate_split, precision=lax.Precision.HIGHEST).astype(jnp.bfloat16)
    up_terms = jnp.einsum('rtkq,ktqf->rtkf', rows_split, up_split, precision=lax.Precision.HIGHEST).astype(jnp.bfloat16)
    gate = lax.optimization_barrier(jnp.sum(gate_terms.astype(jnp.float32), axis=(1, 2)))
    up_sum = lax.optimization_barrier(jnp.sum(up_terms.astype(jnp.float32), axis=(1, 2)))
    hidden = (jax.nn.silu(gate) * up_sum).astype(jnp.bfloat16)
    down_split = down_weight_couple.astype(jnp.float32).reshape(2, N_SIDE, FF_PART, N_TP, D_QUARTER)
    hidden_split = hidden.astype(jnp.float32).reshape(count, N_SIDE, FF_PART)
    part_out = jnp.einsum('rjf,kjftq->rjtkq', hidden_split, down_split, precision=lax.Precision.HIGHEST).astype(jnp.bfloat16)
    slot_out = lax.optimization_barrier(jnp.sum(part_out.astype(jnp.float32), axis=1)).astype(jnp.bfloat16)
    return slot_out.reshape(count, D)

def reference(queries, key_rows, value_rows, segments, hidden_entry_rows, expert_ids, route_weight, w_gate, w_up, w_down):
    attended = lax.map(attend_sequence, (queries, key_rows, value_rows, segments))
    count = SEQS * SEQ_LEN
    flat_rows = hidden_entry_rows.reshape(count, D)
    flat_ids = expert_ids.reshape(count, TOPK)
    flat_weights = route_weight.reshape(count, TOPK)
    expert_iota = jnp.arange(EXPERTS, dtype=jnp.int32)
    named = flat_ids[:, :, None] == expert_iota[None, None, :]
    hits = lax.optimization_barrier(jnp.sum(named.astype(jnp.int32), axis=1))
    shares = lax.optimization_barrier(jnp.sum(jnp.where(named, flat_weights[:, :, None], 0.0), axis=1))
    blocked = hits.reshape(count // TOK_DEV, TOK_DEV, EXPERTS)
    ranks = (jnp.cumsum(blocked, axis=1) - blocked).reshape(count, EXPERTS)
    slots_all = SEQS * N_BLK * CAP
    owners = jnp.arange(count, dtype=jnp.int32) // TOK_DEV
    slot_of = jnp.where(hits > 0, owners[:, None] * CAP + ranks, slots_all).astype(jnp.int32)
    padded_rows = jnp.concatenate([flat_rows, jnp.zeros((1, D), flat_rows.dtype)], 0)
    token_iota = jnp.arange(count, dtype=jnp.int32)

    def one_expert(output, expert):
        slot_column = lax.dynamic_index_in_dim(slot_of, expert, 1, keepdims=False)
        share_column = lax.dynamic_index_in_dim(shares, expert, 1, keepdims=False)
        token_of_slot = jnp.full((slots_all + 1,), count, jnp.int32).at[slot_column].set(token_iota)[:slots_all]
        weight_of_slot = jnp.zeros((slots_all + 1,), jnp.float32).at[slot_column].set(share_column)[:slots_all]
        rows = padded_rows[token_of_slot]
        gate_pair = jnp.stack([w_gate[expert], w_gate[expert + EXPERTS]])
        up_pair = jnp.stack([w_up[expert], w_up[expert + EXPERTS]])
        down_weight_couple = jnp.stack([w_down[expert], w_down[expert + EXPERTS]])
        combined = expert_pair(rows, gate_pair, up_pair, down_weight_couple).astype(jnp.float32)
        output = output.at[token_of_slot].add(weight_of_slot[:, None] * combined)
        return (output, None)
    initial_running_sum = jnp.zeros((count + 1, D), jnp.float32)
    total_sum, _ = lax.scan(one_expert, initial_running_sum, expert_iota)
    moe_out = total_sum[:count].astype(jnp.bfloat16).reshape(SEQS, SEQ_LEN, D)
    return (attended, moe_out)
```

```python
import functools
import math

import jax
import jax.numpy as jnp
from jax import lax
from jax.experimental import pallas as pl
from jax.experimental.pallas import tpu as pltpu
from jax.sharding import PartitionSpec as P

HEAD_DIM = 128
CAP = 10
PAD = 16
BF = jnp.bfloat16
F32 = jnp.float32
MESH = pl.DeviceIdType.MESH


def iota(shape, dim):
    return lax.broadcasted_iota(jnp.int32, shape, dim)


def dot(a, b):
    return jnp.dot(a, b, preferred_element_type=F32)


def kernel(
    nblk, nside,
    q_hbm, k_hbm, v_hbm, seg_ref, x_hbm, ids_ref, rw_ref, wg_hbm, wu_hbm, wd_hbm,
    att_hbm, moe_hbm,
    q_ref, kv, segs, x_ref, wg, wu, wd, att, moe,
    disp, xin, terms, terms_in, zs, zin, hid, po, pin, rs, rin,
    in_sem, out_sem,
    kv_ss, kv_rs, sg_ss, sg_rs, d_ss, d_rs, f_ss, f_rs, t_ss, t_rs, z_ss, z_rs,
    h_ss, h_rs, p_ss, p_rs, r_ss, r_rs,
):
    experts = nblk // 2
    b = lax.axis_index("blk")
    j = lax.axis_index("side")
    t = lax.axis_index("tp")
    length = q_ref.shape[0]
    heads = q_ref.shape[1] // HEAD_DIM
    quarter = x_ref.shape[1] // 2
    rp = po.shape[1]
    half = nside // 2

    def remote(src, dst, ss, rs_, **where):
        return pltpu.make_async_remote_copy(
            src_ref=src, dst_ref=dst, send_sem=ss, recv_sem=rs_,
            device_id=where, device_id_type=MESH,
        )

    def at_blk(d):
        return lax.rem(b + d, nblk)

    def at_side(d):
        return lax.rem(j + d, nside)

    loads = [
        pltpu.make_async_copy(x_hbm, x_ref, in_sem.at[0]),
        pltpu.make_async_copy(k_hbm, kv.at[b, 0], in_sem.at[1]),
        pltpu.make_async_copy(v_hbm, kv.at[b, 1], in_sem.at[2]),
        pltpu.make_async_copy(wg_hbm, wg, in_sem.at[3]),
        pltpu.make_async_copy(wu_hbm, wu, in_sem.at[4]),
        pltpu.make_async_copy(q_hbm, q_ref, in_sem.at[5]),
        pltpu.make_async_copy(wd_hbm, wd, in_sem.at[6]),
    ]
    for load in loads:
        load.start()

    barrier = pltpu.get_barrier_semaphore()
    for d in range(1, nblk):
        pl.semaphore_signal(barrier, inc=1, device_id={"blk": at_blk(d)}, device_id_type=MESH)
    for d in range(1, nside):
        pl.semaphore_signal(barrier, inc=1, device_id={"side": at_side(d)}, device_id_type=MESH)
    pl.semaphore_signal(barrier, inc=1, device_id={"tp": 1 - t}, device_id_type=MESH)

    ids = ids_ref[...]
    rw = rw_ref[...]
    ep = -(-experts // 8) * 8
    expert_of = iota((ep, length), 0)
    hits = jnp.zeros((ep, length), F32)
    shares = jnp.zeros((ep, length), F32)
    for p in range(ids.shape[0]):
        named = ids[p : p + 1, :] == expert_of
        hits = hits + jnp.where(named, 1.0, 0.0)
        shares = shares + jnp.where(named, rw[p : p + 1, :], 0.0)
    before = jnp.where(iota((length, length), 0) < iota((length, length), 1), 1.0, 0.0)
    ranks = dot(hits.astype(BF), before.astype(BF))
    level = iota((PAD, length), 0).astype(F32)
    picks, pulls = [], []
    for e in range(experts):
        chosen = (hits[e : e + 1, :] > 0.0) & (ranks[e : e + 1, :] == level)
        picks.append(jnp.where(chosen, 1.0, 0.0))
        pulls.append(jnp.where(chosen, shares[e : e + 1, :], 0.0))
    pick = jnp.concatenate(picks, axis=0)
    pull = jnp.concatenate(pulls, axis=0)
    segs[b] = seg_ref[...]
    loads[0].wait()
    taken = dot(pick.astype(BF), x_ref[...]).astype(BF)
    for s in range(nblk):
        e, k = s % experts, s // experts
        disp[s] = taken[e * PAD : (e + 1) * PAD, k * quarter : (k + 1) * quarter]
    xin[j, b] = disp[b]

    loads[1].wait()
    loads[2].wait()
    pl.semaphore_wait(barrier, nblk - 1 + nside - 1 + 1)

    sends = []
    for d in range(1, nblk):
        to = at_blk(d)
        copy = remote(disp.at[to], xin.at[j, b], d_ss.at[d], d_rs.at[b], blk=to)
        copy.start()
        sends.append(copy)
    for d in range(1, nside):
        to = at_side(d)
        copy = remote(xin.at[j, b], xin.at[j, b], f_ss.at[d, 0], f_rs.at[j, b], side=to)
        copy.start()
        sends.append(copy)

    def kv_copy(d):
        to = jnp.minimum(b + d, nblk - 1)
        return (
            remote(kv.at[b], kv.at[b], kv_ss.at[d], kv_rs.at[b], blk=to),
            remote(segs.at[b], segs.at[b], sg_ss.at[d], sg_rs.at[b], blk=to),
        )

    for d in range(1, nblk):
        @pl.when(b + d < nblk)
        def _():
            for copy in kv_copy(d):
                copy.start()

    for d in range(1, nblk):
        @pl.when(b + d < nblk)
        def _():
            kv[b + d] = jnp.zeros(kv.shape[1:], kv.dtype)
            segs[b + d] = jnp.zeros(segs.shape[1:], segs.dtype)

    order = []
    for step in range(1, nblk // 2 + 1):
        for d in (step, nblk - step):
            if d not in order:
                order.append(d)
    for d in order:
        source = at_blk(d)
        remote(disp.at[0], xin.at[j, source], d_ss.at[0], d_rs.at[source], blk=source).wait_recv()
        for d2 in range(1, nside):
            to = at_side(d2)
            copy = remote(
                xin.at[j, source], xin.at[j, source], f_ss.at[d2, d], f_rs.at[j, source], side=to
            )
            copy.start()
            sends.append(copy)

    m = iota((rp, nblk * PAD), 1)
    low = m & (PAD - 1)
    packed = (low < CAP) & ((m >> 4) * CAP + low == iota((rp, nblk * PAD), 0))
    pack = jnp.where(packed, 1.0, 0.0).astype(BF)
    r = iota((nblk * PAD, rp), 0)
    low = r & (PAD - 1)
    spread = (low < CAP) & ((r >> 4) * CAP + low == iota((nblk * PAD, rp), 1))
    unpack = jnp.where(spread, 1.0, 0.0).astype(BF)

    for d2 in range(1, nside):
        other = at_side(d2)
        for d in range(nblk):
            source = at_blk(d)
            remote(
                xin.at[other, source], xin.at[other, source], f_ss.at[0, 0],
                f_rs.at[other, source], side=other,
            ).wait_recv()
    rows = jnp.concatenate(
        [
            dot(pack, xin[s].reshape(nblk * PAD, quarter)).astype(BF)
            for s in range(nside)
        ],
        axis=0,
    )
    loads[3].wait()
    gate = dot(rows, wg[...]).astype(BF)
    for s in range(nside):
        terms[s, 0] = gate[s * rp : (s + 1) * rp]
    loads[4].wait()
    up = dot(rows, wu[...]).astype(BF)
    for s in range(nside):
        terms[s, 1] = up[s * rp : (s + 1) * rp]

    mine = pl.ds(t * half, half)
    theirs = pl.ds((1 - t) * half, half)
    copy = remote(terms.at[theirs], terms_in, t_ss, t_rs, tp=1 - t)
    copy.start()
    copy.wait()
    zs[...] = (terms[mine].astype(F32) + terms_in[...].astype(F32)).astype(BF)
    z_copy = remote(zs, zin, z_ss, z_rs, blk=at_blk(experts))
    z_copy.start()

    for d in range(1, nblk):
        @pl.when(b - d >= 0)
        def _():
            source = jnp.maximum(b - d, 0)
            remote(kv.at[source], kv.at[source], kv_ss.at[0], kv_rs.at[source], blk=source).wait_recv()
            remote(segs.at[source], segs.at[source], sg_ss.at[0], sg_rs.at[source], blk=source).wait_recv()
    loads[5].wait()
    keys_all = nblk * length
    seg_keys = jnp.concatenate([segs[s] for s in range(nblk)], axis=1)
    seg_own = jnp.broadcast_to(segs[b].astype(F32), (length, length)).T
    seg_col = seg_own[:, :1].astype(jnp.int32)
    allowed = (iota((length, keys_all), 1) <= b * length + iota((length, keys_all), 0)) & (
        seg_keys == seg_col
    )
    factor = 1.0 / math.sqrt(HEAD_DIM)
    key_all = kv[:, 0].reshape(keys_all, HEAD_DIM)
    value_all = kv[:, 1].reshape(keys_all, HEAD_DIM)
    unroll = 4 if nblk <= 8 else 1

    def some_heads(step, carry):
        for u in range(unroll):
            cols = pl.ds(pl.multiple_of((step * unroll + u) * HEAD_DIM, HEAD_DIM), HEAD_DIM)
            scores = lax.dot_general(
                q_ref[:, cols], key_all, (((1,), (1,)), ((), ())), preferred_element_type=F32
            )
            scores = jnp.where(allowed, scores * factor, -1e30)
            largest = jnp.max(scores, axis=1, keepdims=True)
            weights = jnp.exp(scores - largest)
            totals = jnp.sum(weights, axis=1, keepdims=True)
            att[:, cols] = (dot(weights.astype(BF), value_all) / totals).astype(BF)
        return carry

    lax.fori_loop(0, heads // unroll, some_heads, 0)
    att_out = pltpu.make_async_copy(att, att_hbm, out_sem.at[0])
    att_out.start()

    z_copy.wait()
    gate_sum = zs[:, 0].astype(F32) + zin[:, 0].astype(F32)
    up_sum = zs[:, 1].astype(F32) + zin[:, 1].astype(F32)
    hid[mine] = (jax.nn.silu(gate_sum) * up_sum).astype(BF)
    copy = remote(hid.at[mine], hid.at[mine], h_ss, h_rs, tp=1 - t)
    copy.start()
    loads[6].wait()
    copy.wait_send()
    remote(hid.at[theirs], hid.at[theirs], h_ss, h_rs, tp=1 - t).wait_recv()

    for d in range(1, nside):
        to = at_side(d)
        po[to] = dot(hid[to], wd[...]).astype(BF)
        copy = remote(po.at[to], pin.at[j], p_ss.at[d], p_rs.at[j], side=to)
        copy.start()
        sends.append(copy)
    total = dot(hid[j], wd[...]).astype(BF).astype(F32)
    for d in range(1, nside):
        source = at_side(d)
        remote(po.at[0], pin.at[source], p_ss.at[0], p_rs.at[source], side=source).wait_recv()
        total = total + pin[source].astype(F32)
    rs[...] = dot(unpack, total.astype(BF)).astype(BF).reshape(rs.shape)
    for d in range(1, nblk):
        to = at_blk(d)
        copy = remote(rs.at[to], rin.at[b], r_ss.at[d], r_rs.at[b], blk=to)
        copy.start()
        sends.append(copy)
    rin[b] = rs[b]

    width = -(-experts * PAD // 128) * 128
    if width > experts * PAD:
        pull = jnp.concatenate([pull, jnp.zeros((width - experts * PAD, length), F32)], axis=0)
    pull = pull.T[:, : experts * PAD]
    pull_a = pull.astype(BF)
    rest = pull - pull_a.astype(F32)
    pull_b = rest.astype(BF)
    pull_c = (rest - pull_b.astype(F32)).astype(BF)

    for d in order:
        source = at_blk(d)
        remote(rs.at[0], rin.at[source], r_ss.at[0], r_rs.at[source], blk=source).wait_recv()
    for k in range(2):
        back = rin[k * experts : (k + 1) * experts].reshape(experts * PAD, quarter)
        mixed = dot(pull_a, back) + dot(pull_b, back) + dot(pull_c, back)
        moe[:, k * quarter : (k + 1) * quarter] = mixed.astype(BF)
    moe_out = pltpu.make_async_copy(moe, moe_hbm, out_sem.at[1])
    moe_out.start()

    for copy in sends:
        copy.wait_send()
    for d in range(1, nblk):
        @pl.when(b + d < nblk)
        def _():
            for copy in kv_copy(d):
                copy.wait_send()
    att_out.wait()
    moe_out.wait()


def body(
    nblk, nside,
    queries, key_rows, value_rows, segments, hidden_entry_rows, expert_ids, route_weight,
    w_gate, w_up, w_down,
):
    length, width = queries.shape[1:]
    quarter, ff = w_gate.shape[1:]
    rp = -(-nblk * CAP // PAD) * PAD
    half = nside // 2
    vmem = pl.BlockSpec(memory_space=pltpu.VMEM)
    hbm = pl.BlockSpec(memory_space=pl.ANY)
    dma = pltpu.SemaphoreType.DMA
    attended, moe_out = pl.pallas_call(
        functools.partial(kernel, nblk, nside),
        out_shape=(
            jax.ShapeDtypeStruct((length, width), BF),
            jax.ShapeDtypeStruct((length, 2 * quarter), BF),
        ),
        in_specs=[hbm, hbm, hbm, vmem, hbm, vmem, vmem, hbm, hbm, hbm],
        out_specs=(hbm, hbm),
        scratch_shapes=[
            pltpu.VMEM((length, width), BF),
            pltpu.VMEM((nblk, 2, length, HEAD_DIM), BF),
            pltpu.VMEM((nblk, 1, length), jnp.int32),
            pltpu.VMEM((length, 2 * quarter), BF),
            pltpu.VMEM((quarter, ff), BF),
            pltpu.VMEM((quarter, ff), BF),
            pltpu.VMEM((ff, quarter), BF),
            pltpu.VMEM((length, width), BF),
            pltpu.VMEM((length, 2 * quarter), BF),
            pltpu.VMEM((nblk, PAD, quarter), BF),
            pltpu.VMEM((nside, nblk, PAD, quarter), BF),
            pltpu.VMEM((nside, 2, rp, ff), BF),
            pltpu.VMEM((half, 2, rp, ff), BF),
            pltpu.VMEM((half, 2, rp, ff), BF),
            pltpu.VMEM((half, 2, rp, ff), BF),
            pltpu.VMEM((nside, rp, ff), BF),
            pltpu.VMEM((nside, rp, quarter), BF),
            pltpu.VMEM((nside, rp, quarter), BF),
            pltpu.VMEM((nblk, PAD, quarter), BF),
            pltpu.VMEM((nblk, PAD, quarter), BF),
            dma((7,)),
            dma((2,)),
            dma((nblk,)), dma((nblk,)),
            dma((nblk,)), dma((nblk,)),
            dma((nblk,)), dma((nblk,)),
            dma((nside, nblk)), dma((nside, nblk)),
            dma, dma, dma, dma, dma, dma,
            dma((nside,)), dma((nside,)),
            dma((nblk,)), dma((nblk,)),
        ],
        compiler_params=pltpu.CompilerParams(
            collective_id=0, has_side_effects=True, vmem_limit_bytes=56 * 1024 * 1024
        ),
    )(
        queries[0], key_rows[0], value_rows[0], segments, hidden_entry_rows[0],
        jnp.swapaxes(expert_ids[0], 0, 1), jnp.swapaxes(route_weight[0], 0, 1),
        w_gate[0], w_up[0], w_down[0],
    )
    return attended[None], moe_out[None]


def solution(mesh):
    rows = P(("groups", "side"), "blk", "tp")
    placed = (
        rows, rows, rows,
        P(("groups", "side"), "blk"),
        rows,
        P(("groups", "side"), "blk", None),
        P(("groups", "side"), "blk", None),
        P("blk", "tp", "side"),
        P("blk", "tp", "side"),
        P("blk", "side", "tp"),
    )
    return jax.shard_map(
        functools.partial(body, mesh.shape["blk"], mesh.shape["side"]),
        mesh=mesh,
        in_specs=placed,
        out_specs=(rows, rows),
        check_vma=False,
    )
```

```python
import functools
import math

import jax
import jax.numpy as jnp
from jax import lax
from jax.experimental import pallas as pl
from jax.experimental.pallas import tpu as pltpu
from jax.sharding import PartitionSpec as P

HEAD_DIM = 128
CAP = 10
PAD = 16
BF = jnp.bfloat16
F32 = jnp.float32
MESH = pl.DeviceIdType.MESH


def iota(shape, dim):
    return lax.broadcasted_iota(jnp.int32, shape, dim)


def dot(a, b):
    return jnp.dot(a, b, preferred_element_type=F32)


def cuts(width):
    first = (width // 128 + 1) // 2 * 128
    return pl.ds(0, first), pl.ds(first, width - first)


def kernel(
    nblk, nside,
    q_hbm, k_hbm, v_hbm, seg_ref, x_hbm, ids_ref, rw_ref, wg_hbm, wu_hbm, wd_hbm,
    att_hbm, rin, pull_hbm,
    q_ref, kv, segs, x_ref, wg, wu, wd, att, pull_ref,
    disp, xin, terms, terms_in, zs, zin, hid, po, pin, rs,
    in_sem, out_sem,
    kv_ss, kv_rs, sg_ss, sg_rs, d_ss, d_rs, f_ss, f_rs, t_ss, t_rs, z_ss, z_rs,
    h_ss, h_rs, p_ss, p_rs, r_ss, r_rs,
):
    experts = nblk // 2
    b = lax.axis_index("blk")
    j = lax.axis_index("side")
    t = lax.axis_index("tp")
    length = q_ref.shape[0]
    heads = q_ref.shape[1] // HEAD_DIM
    quarter = x_ref.shape[1] // 2
    rp = po.shape[1]
    half = nside // 2
    hidden_cuts = cuts(wg.shape[1])
    out_cuts = cuts(quarter)

    def remote(src, dst, ss, rs_, **where):
        return pltpu.make_async_remote_copy(
            src_ref=src, dst_ref=dst, send_sem=ss, recv_sem=rs_,
            device_id=where, device_id_type=MESH,
        )

    def at_blk(d):
        return lax.rem(b + d, nblk)

    def at_side(d):
        return lax.rem(j + d, nside)

    loads = [
        pltpu.make_async_copy(x_hbm, x_ref, in_sem.at[0]),
        pltpu.make_async_copy(k_hbm, kv.at[b, 0], in_sem.at[1]),
        pltpu.make_async_copy(v_hbm, kv.at[b, 1], in_sem.at[2]),
        pltpu.make_async_copy(wg_hbm, wg, in_sem.at[3]),
        pltpu.make_async_copy(wu_hbm, wu, in_sem.at[4]),
        pltpu.make_async_copy(q_hbm, q_ref, in_sem.at[5]),
        pltpu.make_async_copy(wd_hbm, wd, in_sem.at[6]),
    ]
    for load in loads:
        load.start()

    barrier = pltpu.get_barrier_semaphore()
    for d in range(1, nblk):
        pl.semaphore_signal(barrier, inc=1, device_id={"blk": at_blk(d)}, device_id_type=MESH)
    for d in range(1, nside):
        pl.semaphore_signal(barrier, inc=1, device_id={"side": at_side(d)}, device_id_type=MESH)
    pl.semaphore_signal(barrier, inc=1, device_id={"tp": 1 - t}, device_id_type=MESH)

    ids = ids_ref[...]
    rw = rw_ref[...]
    ep = -(-experts // 8) * 8
    expert_of = iota((ep, length), 0)
    hits = jnp.zeros((ep, length), F32)
    shares = jnp.zeros((ep, length), F32)
    for p in range(ids.shape[0]):
        named = ids[p : p + 1, :] == expert_of
        hits = hits + jnp.where(named, 1.0, 0.0)
        shares = shares + jnp.where(named, rw[p : p + 1, :], 0.0)
    before = jnp.where(iota((length, length), 0) < iota((length, length), 1), 1.0, 0.0)
    ranks = dot(hits.astype(BF), before.astype(BF))
    level = iota((PAD, length), 0).astype(F32)
    picks, pulls = [], []
    for e in range(experts):
        chosen = (hits[e : e + 1, :] > 0.0) & (ranks[e : e + 1, :] == level)
        picks.append(jnp.where(chosen, 1.0, 0.0))
        pulls.append(jnp.where(chosen, shares[e : e + 1, :], 0.0))
    pick = jnp.concatenate(picks, axis=0)
    pull_ref[...] = jnp.concatenate(pulls, axis=0)
    pull_out = pltpu.make_async_copy(pull_ref, pull_hbm, out_sem.at[2])
    pull_out.start()
    segs[b] = seg_ref[...]
    loads[0].wait()
    taken = dot(pick.astype(BF), x_ref[...]).astype(BF)
    for s in range(nblk):
        e, k = s % experts, s // experts
        disp[s] = taken[e * PAD : e * PAD + CAP, k * quarter : (k + 1) * quarter]
    xin[j, b] = disp[b]

    loads[1].wait()
    loads[2].wait()
    pl.semaphore_wait(barrier, nblk - 1 + nside - 1 + 1)

    sends = []
    for d in range(1, nblk):
        to = at_blk(d)
        copy = remote(disp.at[to], xin.at[j, b], d_ss.at[d], d_rs.at[b], blk=to)
        copy.start()
        sends.append(copy)
    for d in range(1, nside):
        to = at_side(d)
        copy = remote(xin.at[j, b], xin.at[j, b], f_ss.at[d, 0], f_rs.at[j, b], side=to)
        copy.start()
        sends.append(copy)

    def kv_copy(d):
        to = jnp.minimum(b + d, nblk - 1)
        return (
            remote(kv.at[b], kv.at[b], kv_ss.at[d], kv_rs.at[b], blk=to),
            remote(segs.at[b], segs.at[b], sg_ss.at[d], sg_rs.at[b], blk=to),
        )

    for d in range(1, nblk):
        @pl.when(b + d < nblk)
        def _():
            for copy in kv_copy(d):
                copy.start()

    for d in range(1, nblk):
        @pl.when(b + d < nblk)
        def _():
            kv[b + d] = jnp.zeros(kv.shape[1:], kv.dtype)
            segs[b + d] = jnp.zeros(segs.shape[1:], segs.dtype)

    order = []
    for step in range(1, nblk // 2 + 1):
        for d in (step, nblk - step):
            if d not in order:
                order.append(d)
    for d in order:
        source = at_blk(d)
        remote(disp.at[0], xin.at[j, source], d_ss.at[0], d_rs.at[source], blk=source).wait_recv()
        for d2 in range(1, nside):
            to = at_side(d2)
            copy = remote(
                xin.at[j, source], xin.at[j, source], f_ss.at[d2, d], f_rs.at[j, source], side=to
            )
            copy.start()
            sends.append(copy)

    for d2 in range(1, nside):
        other = at_side(d2)
        for d in range(nblk):
            source = at_blk(d)
            remote(
                xin.at[other, source], xin.at[other, source], f_ss.at[0, 0],
                f_rs.at[other, source], side=other,
            ).wait_recv()
    rows = jnp.concatenate([xin[s, i] for s in range(nside) for i in range(nblk)], axis=0)
    mine = pl.ds(t * half, half)
    theirs = pl.ds((1 - t) * half, half)
    loads[3].wait()
    loads[4].wait()
    t_copies, z_copies, h_copies = [], [], []
    for c, cols in enumerate(hidden_cuts):
        gate = dot(rows, wg[:, cols]).astype(BF)
        up = dot(rows, wu[:, cols]).astype(BF)
        for s in range(nside):
            terms[s, 0, :, cols] = gate[s * rp : (s + 1) * rp]
            terms[s, 1, :, cols] = up[s * rp : (s + 1) * rp]
        t_copies.append(remote(
            terms.at[theirs, :, :, cols], terms_in.at[:, :, :, cols], t_ss.at[c], t_rs.at[c], tp=1 - t
        ))
        t_copies[c].start()
    for c, cols in enumerate(hidden_cuts):
        t_copies[c].wait()
        zs[:, :, :, cols] = (
            terms[mine, :, :, cols].astype(F32) + terms_in[:, :, :, cols].astype(F32)
        ).astype(BF)
        z_copies.append(remote(
            zs.at[:, :, :, cols], zin.at[:, :, :, cols], z_ss.at[c], z_rs.at[c], blk=at_blk(experts)
        ))
        z_copies[c].start()

    for d in range(1, nblk):
        @pl.when(b - d >= 0)
        def _():
            source = jnp.maximum(b - d, 0)
            remote(kv.at[source], kv.at[source], kv_ss.at[0], kv_rs.at[source], blk=source).wait_recv()
            remote(segs.at[source], segs.at[source], sg_ss.at[0], sg_rs.at[source], blk=source).wait_recv()
    loads[5].wait()
    keys_all = nblk * length
    seg_keys = jnp.concatenate([segs[s] for s in range(nblk)], axis=1)
    seg_own = jnp.broadcast_to(segs[b].astype(F32), (length, length)).T
    seg_col = seg_own[:, :1].astype(jnp.int32)
    allowed = (iota((length, keys_all), 1) <= b * length + iota((length, keys_all), 0)) & (
        seg_keys == seg_col
    )
    factor = 1.0 / math.sqrt(HEAD_DIM)
    key_all = kv[:, 0].reshape(keys_all, HEAD_DIM)
    value_all = kv[:, 1].reshape(keys_all, HEAD_DIM)
    unroll = 4 if nblk <= 8 else 1

    def some_heads(step, carry):
        for u in range(unroll):
            cols = pl.ds(pl.multiple_of((step * unroll + u) * HEAD_DIM, HEAD_DIM), HEAD_DIM)
            scores = lax.dot_general(
                q_ref[:, cols], key_all, (((1,), (1,)), ((), ())), preferred_element_type=F32
            )
            scores = jnp.where(allowed, scores * factor, -1e30)
            largest = jnp.max(scores, axis=1, keepdims=True)
            weights = jnp.exp(scores - largest)
            totals = jnp.sum(weights, axis=1, keepdims=True)
            att[:, cols] = (dot(weights.astype(BF), value_all) / totals).astype(BF)
        return carry

    lax.fori_loop(0, heads // unroll, some_heads, 0)
    att_out = pltpu.make_async_copy(att, att_hbm, out_sem.at[0])
    att_out.start()

    for c, cols in enumerate(hidden_cuts):
        z_copies[c].wait()
        gate_sum = zs[:, 0, :, cols].astype(F32) + zin[:, 0, :, cols].astype(F32)
        up_sum = zs[:, 1, :, cols].astype(F32) + zin[:, 1, :, cols].astype(F32)
        hid[mine, :, cols] = (jax.nn.silu(gate_sum) * up_sum).astype(BF)
        h_copies.append(remote(
            hid.at[mine, :, cols], hid.at[mine, :, cols], h_ss.at[c], h_rs.at[c], tp=1 - t
        ))
        h_copies[c].start()
    loads[6].wait()
    for c, cols in enumerate(hidden_cuts):
        h_copies[c].wait_send()
        remote(
            hid.at[theirs, :, cols], hid.at[theirs, :, cols], h_ss.at[c], h_rs.at[c], tp=1 - t
        ).wait_recv()

    for c, cols in enumerate(out_cuts):
        for d in range(1, nside):
            to = at_side(d)
            po[to, :, cols] = dot(hid[to], wd[:, cols]).astype(BF)
            copy = remote(
                po.at[to, :, cols], pin.at[j, :, cols], p_ss.at[d, c], p_rs.at[j, c], side=to
            )
            copy.start()
            sends.append(copy)
    totals = [dot(hid[j], wd[:, cols]).astype(BF).astype(F32) for cols in out_cuts]
    for c, cols in enumerate(out_cuts):
        total = totals[c]
        for d in range(1, nside):
            source = at_side(d)
            remote(
                po.at[0, :, cols], pin.at[source, :, cols], p_ss.at[0, c], p_rs.at[source, c], side=source
            ).wait_recv()
            total = total + pin[source, :, cols].astype(F32)
        slot_out = total.astype(BF)
        for s in range(nblk):
            rs[s, :, cols] = slot_out[s * CAP : (s + 1) * CAP]
        for d in order:
            to = at_blk(d)
            copy = remote(
                rs.at[to, :, cols], rin.at[b, :, cols], r_ss.at[d, c], r_rs.at[b, c], blk=to
            )
            copy.start()
            sends.append(copy)
    own_back = pltpu.make_async_copy(rs.at[b], rin.at[b], out_sem.at[1])
    own_back.start()
    for d in order:
        source = at_blk(d)
        for c, cols in enumerate(out_cuts):
            remote(
                rs.at[0, :, cols], rin.at[source, :, cols], r_ss.at[0, c], r_rs.at[source, c], blk=source
            ).wait_recv()
    for copy in sends:
        copy.wait_send()
    for d in range(1, nblk):
        @pl.when(b + d < nblk)
        def _():
            for copy in kv_copy(d):
                copy.wait_send()
    att_out.wait()
    own_back.wait()
    pull_out.wait()


def finish(att_hbm, back_hbm, pull_hbm, out_hbm, moe_hbm, att, back, pull_ref, moe, in_sem, out_sem):
    loads = [
        pltpu.make_async_copy(back_hbm, back, in_sem.at[0]),
        pltpu.make_async_copy(pull_hbm, pull_ref, in_sem.at[1]),
        pltpu.make_async_copy(att_hbm, att, in_sem.at[2]),
    ]
    for load in loads:
        load.start()
    nblk, _, quarter = back.shape
    rows, length = pull_ref.shape
    loads[1].wait()
    pull = pull_ref[...]
    width = -(-rows // 128) * 128
    if width > rows:
        pull = jnp.concatenate([pull, jnp.zeros((width - rows, length), F32)], axis=0)
    pull = pull.T[:, :rows]
    pull_a = pull.astype(BF)
    rest = pull - pull_a.astype(F32)
    pull_b = rest.astype(BF)
    pull_c = (rest - pull_b.astype(F32)).astype(BF)
    pull = jnp.concatenate([pull_a, pull_b, pull_c], axis=1)
    loads[2].wait()
    stores = [pltpu.make_async_copy(att, out_hbm, out_sem.at[0])]
    stores[0].start()
    loads[0].wait()
    experts = nblk // 2
    for k in range(2):
        gap = jnp.zeros((PAD - CAP, quarter), BF)
        one = jnp.concatenate(
            [piece for e in range(experts) for piece in (back[k * experts + e], gap)], axis=0
        )
        cols = pl.ds(k * quarter, quarter)
        moe[:, cols] = dot(pull, jnp.concatenate([one] * 3, axis=0)).astype(BF)
        stores.append(pltpu.make_async_copy(moe.at[:, cols], moe_hbm.at[:, cols], out_sem.at[1 + k]))
        stores[-1].start()
    for store in stores:
        store.wait()


def body(
    nblk, nside,
    queries, key_rows, value_rows, segments, hidden_entry_rows, expert_ids, route_weight,
    w_gate, w_up, w_down,
):
    length, width = queries.shape[1:]
    quarter, ff = w_gate.shape[1:]
    rp = -(-nblk * CAP // 8) * 8
    half = nside // 2
    vmem = pl.BlockSpec(memory_space=pltpu.VMEM)
    hbm = pl.BlockSpec(memory_space=pl.ANY)
    dma = pltpu.SemaphoreType.DMA
    experts = nblk // 2
    part_att, back, pull = pl.pallas_call(
        functools.partial(kernel, nblk, nside),
        out_shape=(
            jax.ShapeDtypeStruct((length, width), BF),
            jax.ShapeDtypeStruct((nblk, CAP, quarter), BF),
            jax.ShapeDtypeStruct((experts * PAD, length), F32),
        ),
        in_specs=[hbm, hbm, hbm, vmem, hbm, vmem, vmem, hbm, hbm, hbm],
        out_specs=(hbm, hbm, hbm),
        scratch_shapes=[
            pltpu.VMEM((length, width), BF),
            pltpu.VMEM((nblk, 2, length, HEAD_DIM), BF),
            pltpu.VMEM((nblk, 1, length), jnp.int32),
            pltpu.VMEM((length, 2 * quarter), BF),
            pltpu.VMEM((quarter, ff), BF),
            pltpu.VMEM((quarter, ff), BF),
            pltpu.VMEM((ff, quarter), BF),
            pltpu.VMEM((length, width), BF),
            pltpu.VMEM((experts * PAD, length), F32),
            pltpu.VMEM((nblk, CAP, quarter), BF),
            pltpu.VMEM((nside, nblk, CAP, quarter), BF),
            pltpu.VMEM((nside, 2, rp, ff), BF),
            pltpu.VMEM((half, 2, rp, ff), BF),
            pltpu.VMEM((half, 2, rp, ff), BF),
            pltpu.VMEM((half, 2, rp, ff), BF),
            pltpu.VMEM((nside, rp, ff), BF),
            pltpu.VMEM((nside, rp, quarter), BF),
            pltpu.VMEM((nside, rp, quarter), BF),
            pltpu.VMEM((nblk, CAP, quarter), BF),
            dma((7,)),
            dma((3,)),
            dma((nblk,)), dma((nblk,)),
            dma((nblk,)), dma((nblk,)),
            dma((nblk,)), dma((nblk,)),
            dma((nside, nblk)), dma((nside, nblk)),
            dma((2,)), dma((2,)), dma((2,)), dma((2,)), dma((2,)), dma((2,)),
            dma((nside, 2)), dma((nside, 2)),
            dma((nblk, 2)), dma((nblk, 2)),
        ],
        compiler_params=pltpu.CompilerParams(
            collective_id=0, has_side_effects=True, vmem_limit_bytes=56 * 1024 * 1024
        ),
    )(
        queries[0], key_rows[0], value_rows[0], segments, hidden_entry_rows[0],
        jnp.swapaxes(expert_ids[0], 0, 1), jnp.swapaxes(route_weight[0], 0, 1),
        w_gate[0], w_up[0], w_down[0],
    )
    attended, moe_out = pl.pallas_call(
        finish,
        out_shape=(
            jax.ShapeDtypeStruct((length, width), BF),
            jax.ShapeDtypeStruct((length, 2 * quarter), BF),
        ),
        in_specs=[hbm, hbm, hbm],
        out_specs=(hbm, hbm),
        scratch_shapes=[
            pltpu.VMEM((length, width), BF),
            pltpu.VMEM((nblk, CAP, quarter), BF),
            pltpu.VMEM((experts * PAD, length), F32),
            pltpu.VMEM((length, 2 * quarter), BF),
            dma((3,)),
            dma((3,)),
        ],
        compiler_params=pltpu.CompilerParams(vmem_limit_bytes=60 * 1024 * 1024),
    )(part_att, back, pull)
    return attended[None], moe_out[None]


def solution(mesh):
    rows = P(("groups", "side"), "blk", "tp")
    placed = (
        rows, rows, rows,
        P(("groups", "side"), "blk"),
        rows,
        P(("groups", "side"), "blk", None),
        P(("groups", "side"), "blk", None),
        P("blk", "tp", "side"),
        P("blk", "tp", "side"),
        P("blk", "side", "tp"),
    )
    return jax.shard_map(
        functools.partial(body, mesh.shape["blk"], mesh.shape["side"]),
        mesh=mesh,
        in_specs=placed,
        out_specs=(rows, rows),
        check_vma=False,
    )
```
